32 devices in a mesh: dp: 8 (over z, y), rep: 4 (over x, core).
Axes of the slice: x: 2, y: 2, z: 4, core: 2. Of those that a mesh axis runs over, the one named last changes fastest.
Arguments:
- circuits: bfloat16 [8192, 1024], P(('dp', 'rep')), may hold values from -2.65 to 2.65
- records: bfloat16 [8192, 1024], P(('dp', 'rep')), may hold values from -0.25 to 0.25
- record_gain: float32 [1024], replicated, may hold values from 0.5 to 2
- log_scale: float32 [1], replicated, may hold values from 1.6 to 2.4
- logit_bias: float32 [1], replicated, may hold values from -3 to -1
- hard_ids: int32 [8192, 16], P(('dp', 'rep')), may hold values from -1 to 8191, as said below
Outputs:
- grad_circuits: float32 [8192, 1024], P(('dp', 'rep'))
- grad_records: float32 [8192, 1024], P(('dp', 'rep'))
- grad_gain: float32 [1024], replicated
- statistics: float32 [2], replicated
- mean_loss: float32 [1], replicated
The draws below stay inside these ranges and needn't reach their ends.
Inputs may be any that keep to these rules, and one draw needn't show every extreme that they name: `hard_ids`: every entry that is not -1 names a row held by a device with the same dp index as the pair's device (the same value of row // 1024). Over the 256 pairs of one device, at most 16 entries name rows of any one device, and in each dp index one device is named exactly 16 times by every device of that dp index.
All inputs are finite; a program needn't handle non-finite values.
Results may differ from the reference program's by a relative error of at most 0.0043.
Values may be sent and summed in bfloat16 or wider, within the bound.
A program may use at most 64 MiB of HBM per device.

```python
import math
import jax
import jax.numpy as jnp
from jax import lax

D = 1024
PAIRS_DEV = 256
HOPS = 4
HN = 16
CAP = 16
TOTAL = 8192
N_DP = 8
N_REP = 4


def draw_hard_ids(key, part):
    device_total = N_DP * N_REP
    slot_total = PAIRS_DEV * HN
    load_top = max(CAP * 2 // 3, 1) + 1

    def one_device(device):
        device_key = jax.random.fold_in(jax.random.fold_in(key, 11), device)
        loop_index = device // N_REP
        full_key = jax.random.fold_in(jax.random.fold_in(key, 23), loop_index)
        load_key, rank_key, row_key = jax.random.split(device_key, 3)
        owner_loads = jax.random.randint(load_key, (N_REP,), 1, load_top)
        full_owner = jax.random.randint(full_key, (), 0, N_REP)
        owner_loads = jnp.where(jnp.arange(N_REP) == full_owner, CAP, owner_loads)
        cumulative = jnp.cumsum(owner_loads)
        slot_rank = jax.random.permutation(rank_key, slot_total)
        owner_dev = jnp.sum((cumulative[None, :] <= slot_rank[:, None]).astype(jnp.int32), axis=1)
        is_live = slot_rank < cumulative[-1]
        row_pick = jax.random.randint(row_key, (slot_total,), 0, PAIRS_DEV)
        global_row = (loop_index * N_REP + jnp.minimum(owner_dev, N_REP - 1)) * PAIRS_DEV + row_pick
        return jnp.where(is_live, global_row, -1).reshape(PAIRS_DEV, HN)
    all_devices = jax.vmap(one_device)(jnp.arange(device_total))
    return all_devices.reshape(TOTAL, HN).astype(jnp.int32)


def feature_noise(noise_key):
    values = jax.random.normal(noise_key, (TOTAL, D), jnp.float32) * 0.03125
    return jnp.clip(values, -0.25, 0.25)


def record_values(key):
    return feature_noise(jax.random.fold_in(key, 101))


def draw_records(key, part):
    return record_values(key).astype(jnp.bfloat16)


def draw_circuits(key, part):
    record_rows = record_values(key).astype(jnp.bfloat16).astype(jnp.float32)
    noise = feature_noise(jax.random.fold_in(key, 202))
    id_table = draw_hard_ids(key, part)

    def one_block(id_block):
        is_live = id_block >= 0
        safe_ids = jnp.where(is_live, id_block, 0).astype(jnp.int32)
        picked = jnp.take(record_rows, safe_ids.reshape(-1), axis=0).reshape(PAIRS_DEV, HN, D)
        return jnp.sum(jnp.where(is_live[:, :, None], picked, 0.0), axis=1)
    mined = lax.map(one_block, id_table.reshape(N_DP * N_REP, PAIRS_DEV, HN)).reshape(TOTAL, D)
    return (noise + 0.6 * mined).astype(jnp.bfloat16)


def setup_inputs(seed: int = 0) -> dict:
    streams_of = jax.random.split(jax.random.key(seed), 7)
    return {
        "circuits": draw_circuits(jax.random.fold_in(streams_of[6], 71), 0),
        "records": draw_records(jax.random.fold_in(streams_of[6], 71), 0),
        "record_gain": jnp.clip(jnp.exp(jax.random.uniform(streams_of[2], (D,), jnp.float32, math.log(0.5), math.log(2.0))), 0.5, 2.0),
        "log_scale": jnp.clip(jax.random.uniform(streams_of[3], (1,), jnp.float32, 1.6, 2.4), 1.6, 2.4),
        "logit_bias": jnp.clip(jax.random.uniform(streams_of[4], (1,), jnp.float32, -3.0, -1.0), -3.0, -1.0),
        "hard_ids": draw_hard_ids(jax.random.fold_in(streams_of[6], 71), 0),
    }


EPSILON = 1e-06

def unit_rows(values):
    sq_total = lax.optimization_barrier(jnp.sum(values * values, axis=-1, keepdims=True))
    lengths = jnp.sqrt(sq_total + EPSILON)
    return (values / lengths, lengths)

def rounded(values):
    return lax.optimization_barrier(values.astype(jnp.bfloat16)).astype(jnp.float32)

def reference(circuits, records, record_gain, log_scale, logit_bias, hard_ids):
    circ_unit, circ_length = unit_rows(circuits.astype(jnp.float32))
    circ_emb = circ_unit.astype(jnp.bfloat16)
    rec_pre = records.astype(jnp.float32) * record_gain
    rec_unit, rec_length = unit_rows(rec_pre)
    rec_emb = rec_unit.astype(jnp.bfloat16)
    multiplier = jnp.exp(log_scale[0])
    bias_value = logit_bias[0]
    circ_blocks = circ_emb.astype(jnp.float32).reshape(N_DP, N_REP, PAIRS_DEV, D)
    rec_blocks = rec_emb.astype(jnp.float32).reshape(N_DP, N_REP, PAIRS_DEV, D)
    diag_mask = jnp.eye(PAIRS_DEV, dtype=jnp.float32)
    grad_circ = jnp.zeros((N_DP, N_REP, PAIRS_DEV, D), jnp.float32)
    grad_rec = jnp.zeros((N_DP, N_REP, PAIRS_DEV, D), jnp.float32)
    scale_sum = jnp.zeros((), jnp.float32)
    bias_sum = jnp.zeros((), jnp.float32)
    loss_sum = jnp.zeros((), jnp.float32)
    for hop_index in range(HOPS + 1):
        partner = jnp.roll(rec_blocks, -hop_index, axis=0)
        scores = jnp.einsum('abid,abjd->abij', circ_blocks, partner) * multiplier + bias_value
        weights = jax.nn.sigmoid(scores)
        losses = jax.nn.softplus(scores)
        if hop_index == 0:
            weights = weights - diag_mask
            losses = losses - scores * diag_mask
        scale_sum = scale_sum + jnp.sum(weights * (scores - bias_value))
        bias_sum = bias_sum + jnp.sum(weights)
        loss_sum = loss_sum + jnp.sum(losses)
        narrow = rounded(weights)
        grad_circ = grad_circ + jnp.einsum('abij,abjd->abid', narrow, partner)
        grad_rec = grad_rec + jnp.roll(jnp.einsum('abij,abid->abjd', narrow, circ_blocks), hop_index, axis=0)

    def hard_block(blocks):
        id_block, circ_block = blocks
        is_live = id_block >= 0
        safe_ids = jnp.where(is_live, id_block, 0).astype(jnp.int32)
        fetched = jnp.take(rec_emb, safe_ids.reshape(-1), axis=0).reshape(PAIRS_DEV, HN, D).astype(jnp.float32)
        products = jnp.einsum('ihd,id->ih', fetched, circ_block.astype(jnp.float32))
        hard_scores = products * multiplier + bias_value
        hard_weights = jnp.where(is_live, jax.nn.sigmoid(hard_scores), 0.0)
        hard_losses = jnp.where(is_live, jax.nn.softplus(hard_scores), 0.0)
        contrib = jnp.einsum('ih,ihd->id', rounded(hard_weights), fetched)
        return (contrib, jnp.sum(hard_weights * products * multiplier), jnp.sum(hard_weights), jnp.sum(hard_losses))
    hard_contrib, hard_scale, hard_bias, hard_loss = lax.map(hard_block, (hard_ids.reshape(N_DP * N_REP, PAIRS_DEV, HN), circ_emb.reshape(N_DP * N_REP, PAIRS_DEV, D)))
    grad_circ_emb = multiplier * (grad_circ.reshape(TOTAL, D) + hard_contrib.reshape(TOTAL, D))
    grad_rec_emb = multiplier * grad_rec.reshape(TOTAL, D)
    grad_circuits = (grad_circ_emb - circ_unit * lax.optimization_barrier(jnp.sum(circ_unit * grad_circ_emb, axis=-1, keepdims=True))) / circ_length
    grad_pre = (grad_rec_emb - rec_unit * lax.optimization_barrier(jnp.sum(rec_unit * grad_rec_emb, axis=-1, keepdims=True))) / rec_length
    grad_records = grad_pre * record_gain
    grad_gain = lax.optimization_barrier(jnp.sum(records.astype(jnp.float32) * grad_pre, axis=0))
    statistics = jnp.stack([scale_sum + jnp.sum(hard_scale), bias_sum + jnp.sum(hard_bias)])
    mean_loss = jnp.stack([(loss_sum + jnp.sum(hard_loss)) / TOTAL])
    return (grad_circuits, grad_records, grad_gain, statistics, mean_loss)
```

```python
import jax
import jax.numpy as jnp
from jax import lax
from jax.sharding import PartitionSpec as P

HOPS = 4


EPSILON = 1e-06


def shifted(value, axis, steps):
    count = lax.axis_size(axis)
    pairs = [(source, (source + steps) % count) for source in range(count)]
    return lax.ppermute(value, axis, pairs)


def unit_rows(values):
    sq_total = jnp.sum(values * values, axis=-1, keepdims=True)
    lengths = jnp.sqrt(sq_total + EPSILON)
    return (values / lengths, lengths)


def transposed_product(left, right):
    return lax.dot_general(
        left, right, (((0,), (0,)), ((), ())), preferred_element_type=jnp.float32
    )


def score_tile(circ_block, rec_block, multiplier, bias_value, own_block):
    products = lax.dot_general(
        circ_block, rec_block, (((1,), (1,)), ((), ())), preferred_element_type=jnp.float32
    )
    scores = products * multiplier + bias_value
    weights = jax.nn.sigmoid(scores)
    losses = jax.nn.softplus(scores)
    if own_block:
        tile_rows = scores.shape[0]
        diag_mask = (
            lax.broadcasted_iota(jnp.int32, (tile_rows, tile_rows), 0)
            == lax.broadcasted_iota(jnp.int32, (tile_rows, tile_rows), 1)
        ).astype(jnp.float32)
        weights = weights - diag_mask
        losses = losses - scores * diag_mask
    summary = jnp.stack(
        [jnp.sum(weights * (scores - bias_value)), jnp.sum(weights), jnp.sum(losses)]
    )
    return (weights.astype(jnp.bfloat16), summary)


def tile_terms(circ_block, rec_block, multiplier, bias_value):
    products = lax.dot_general(
        circ_block, rec_block, (((1,), (1,)), ((), ())), preferred_element_type=jnp.float32
    )
    return products * multiplier + bias_value


def per_device(circuits, records, record_gain, log_scale, logit_bias, hard_ids):
    pair_rows = circuits.shape[0]
    list_width = hard_ids.shape[1]
    rep_count = lax.axis_size("rep")
    loop_count = lax.axis_size("dp")
    circ_unit, circ_length = unit_rows(circuits.astype(jnp.float32))
    circ_emb = circ_unit.astype(jnp.bfloat16)
    rec_pre = records.astype(jnp.float32) * record_gain
    rec_unit, rec_length = unit_rows(rec_pre)
    rec_emb = rec_unit.astype(jnp.bfloat16)
    multiplier = jnp.exp(log_scale[0])
    bias_value = logit_bias[0]
    even = lax.axis_index("dp") % 2 == 0
    swap = [(source, source ^ 1) for source in range(loop_count)]

    rec2 = shifted(rec_emb, "dp", -2)
    circ2 = shifted(circ_emb, "dp", 2)
    rec4 = shifted(rec2, "dp", -2)
    circ4 = shifted(circ2, "dp", 2)
    rec1 = lax.ppermute(jnp.where(even, rec2, rec_emb), "dp", swap)
    circ1 = lax.ppermute(jnp.where(even, circ_emb, circ2), "dp", swap)
    rec3 = lax.ppermute(jnp.where(even, rec4, rec2), "dp", swap)
    circ3 = lax.ppermute(jnp.where(even, circ2, circ4), "dp", swap)

    own_weights, summary = score_tile(circ_emb, rec_emb, multiplier, bias_value, True)
    grad_circ = jnp.dot(own_weights, rec_emb, preferred_element_type=jnp.float32)
    grad_rec = transposed_product(own_weights, circ_emb)

    everyone = lax.all_gather(rec_emb, "rep", axis=0, tiled=True)
    first_row = (lax.axis_index("dp") * rep_count) * pair_rows
    columns = lax.broadcasted_iota(jnp.int32, (pair_rows, rep_count * pair_rows), 1) + first_row
    times = jnp.zeros(columns.shape, jnp.float32)
    for entry in range(list_width):
        times = times + (hard_ids[:, entry][:, None] == columns).astype(jnp.float32)

    for visitor, guest in ((rec2, circ2), (rec1, circ1), (rec4, circ4), (rec3, circ3)):
        weights, portion = score_tile(circ_emb, visitor, multiplier, bias_value, False)
        grad_circ = grad_circ + jnp.dot(weights, visitor, preferred_element_type=jnp.float32)
        summary = summary + portion
        scores = tile_terms(guest, rec_emb, multiplier, bias_value)
        weights = jax.nn.sigmoid(scores).astype(jnp.bfloat16)
        grad_rec = grad_rec + transposed_product(weights, guest)

    scores = tile_terms(circ_emb, everyone, multiplier, bias_value)
    sigmoids = jax.nn.sigmoid(scores)
    weights = times * sigmoids
    narrow = (times * sigmoids.astype(jnp.bfloat16).astype(jnp.float32)).astype(jnp.bfloat16)
    hard_grad = jnp.dot(narrow, everyone, preferred_element_type=jnp.float32)
    summary = summary + jnp.stack(
        [
            jnp.sum(weights * (scores - bias_value)),
            jnp.sum(weights),
            jnp.sum(times * jax.nn.softplus(scores)),
        ]
    )
    grad_circ_emb = multiplier * (grad_circ + hard_grad)
    grad_rec_emb = multiplier * grad_rec
    grad_circuits = (
        grad_circ_emb - circ_unit * jnp.sum(circ_unit * grad_circ_emb, axis=-1, keepdims=True)
    ) / circ_length
    grad_pre = (
        grad_rec_emb - rec_unit * jnp.sum(rec_unit * grad_rec_emb, axis=-1, keepdims=True)
    ) / rec_length
    grad_records = grad_pre * record_gain
    gain_part = jnp.sum(records.astype(jnp.float32) * grad_pre, axis=0)
    gain_total, summary_total = lax.psum((gain_part, summary), ("dp", "rep"))
    pair_total = pair_rows * loop_count * rep_count
    statistics = jnp.stack([summary_total[0], summary_total[1]])
    mean_loss = jnp.stack([summary_total[2] / pair_total])
    return (grad_circuits, grad_records, gain_total, statistics, mean_loss)


def solution(mesh):
    placed = (P(("dp", "rep"), None), P(("dp", "rep"), None), P(), P(), P(), P(("dp", "rep"), None))
    return jax.shard_map(
        per_device,
        mesh=mesh,
        in_specs=placed,
        out_specs=(P(("dp", "rep"), None), P(("dp", "rep"), None), P(), P(), P()),
        check_vma=False,
    )
```

```python
import functools

import jax
import jax.numpy as jnp
from jax import lax
from jax.experimental import pallas as pl
from jax.experimental.pallas import tpu as pltpu
from jax.sharding import PartitionSpec as P

EPSILON = 1e-06
CHUNKS = 4
REC = 0
CIRC = 5
MESH = pl.DeviceIdType.MESH
NT = (((1,), (1,)), ((), ()))


def kernel(
    loop_count,
    rep_count,
    circ_ref,
    rec_ref,
    gain_ref,
    scale_ref,
    bias_ref,
    ids_ref,
    out_circ,
    out_rec,
    out_gain,
    out_stat,
    out_loss,
    bufs,
    group,
    inv_circ,
    inv_rec,
    sums,
    red_rep,
    red_dp,
    send_sem,
    recv_sem,
    group_send,
    group_recv,
    rep_send,
    rep_recv,
    dp_send,
    dp_recv,
):
    rows = circ_ref.shape[0]
    step = rows // CHUNKS
    me = lax.axis_index("dp")
    my_rep = lax.axis_index("rep")
    odd = me % 2
    even = 1 - odd
    below = (me + loop_count - 2) % loop_count
    above = (me + 2) % loop_count
    partner = me + 1 - 2 * odd

    barrier = pltpu.get_barrier_semaphore()

    @pl.loop(1, loop_count)
    def _(k):
        pl.semaphore_signal(
            barrier, inc=1, device_id={"dp": (me + k) % loop_count}, device_id_type=MESH
        )

    @pl.loop(1, rep_count)
    def _(k):
        pl.semaphore_signal(
            barrier, inc=1, device_id={"rep": (my_rep + k) % rep_count}, device_id_type=MESH
        )

    def piece(slot, c):
        return bufs.at[slot, pl.ds(c * step, step)]

    def transfer(message, source, target, device, c):
        return pltpu.make_async_remote_copy(
            src_ref=piece(source, c),
            dst_ref=piece(target, c),
            send_sem=send_sem.at[message, c],
            recv_sem=recv_sem.at[target, c],
            device_id={"dp": device},
            device_id_type=MESH,
        )

    rec_two = (0, REC, REC + 2, below)
    circ_two = (1, CIRC, CIRC + 2, above)
    rec_four = (2, REC + 2, REC + 4, below)
    circ_four = (3, CIRC + 2, CIRC + 4, above)
    swap_own = (4, even * CIRC, even * (CIRC + 1) + odd * (REC + 1), partner)
    swap_rec = (5, REC + 2, even * (REC + 1) + odd * (REC + 3), partner)
    swap_circ = (6, CIRC + 2, even * (CIRC + 3) + odd * (CIRC + 1), partner)
    swap_last = (
        7,
        even * (REC + 4) + odd * (CIRC + 4),
        even * (REC + 3) + odd * (CIRC + 3),
        partner,
    )
    messages = (
        rec_two,
        circ_two,
        rec_four,
        circ_four,
        swap_own,
        swap_rec,
        swap_circ,
        swap_last,
    )

    def arrived(slot, c):
        transfer(0, slot, slot, partner, c).wait_recv()

    def group_copy(k):
        return pltpu.make_async_remote_copy(
            src_ref=bufs.at[REC],
            dst_ref=group.at[rep_count - k],
            send_sem=group_send.at[k],
            recv_sem=group_recv.at[rep_count - k],
            device_id={"rep": (my_rep + k) % rep_count},
            device_id_type=MESH,
        )

    multiplier = jnp.exp(jnp.full((1, 1), scale_ref[0], jnp.float32))
    bias_value = bias_ref[0]

    pl.semaphore_wait(barrier, loop_count + rep_count - 2)

    for c in range(CHUNKS):
        part = pl.ds(c * step, step)
        values = rec_ref[part].astype(jnp.float32) * gain_ref[...]
        inverse = lax.rsqrt(jnp.sum(values * values, axis=-1, keepdims=True) + EPSILON)
        inv_rec[part] = inverse
        bufs[REC, part] = (values * inverse).astype(jnp.bfloat16)
        transfer(*rec_two, c).start()
        values = circ_ref[part].astype(jnp.float32)
        inverse = lax.rsqrt(jnp.sum(values * values, axis=-1, keepdims=True) + EPSILON)
        inv_circ[part] = inverse
        bufs[CIRC, part] = (values * inverse).astype(jnp.bfloat16)
        transfer(*circ_two, c).start()
        transfer(*swap_own, c).start()

    @pl.loop(1, rep_count)
    def _(k):
        group_copy(k).start()

    group[0] = bufs[REC]
    sums[...] = jnp.zeros_like(sums)

    def add_sums(weights, scores, losses):
        sums[0:1] += jnp.sum(weights * (scores - bias_value), axis=0, keepdims=True)
        sums[1:2] += jnp.sum(weights, axis=0, keepdims=True)
        sums[2:3] += jnp.sum(losses, axis=0, keepdims=True)

    def score(left, right):
        products = lax.dot_general(left, right, NT, preferred_element_type=jnp.float32)
        return products * multiplier + bias_value

    def sigmoid_and_loss(scores):
        small = jnp.exp(-jnp.abs(scores))
        weights = jnp.where(scores >= 0, 1.0, small) / (1.0 + small)
        return weights, jnp.maximum(scores, 0.0) + jnp.log1p(small)

    def diagonal():
        shape = (rows, rows)
        same = lax.broadcasted_iota(jnp.int32, shape, 0) == lax.broadcasted_iota(
            jnp.int32, shape, 1
        )
        return jnp.where(same, 1.0, 0.0)

    def rec_tile(offset):
        other = bufs[REC + offset]
        scores = score(bufs[CIRC], other)
        weights, losses = sigmoid_and_loss(scores)
        if offset == 0:
            mask = diagonal()
            weights = weights - mask
            losses = losses - scores * mask
        add_sums(weights, scores, losses)
        term = jnp.dot(weights.astype(jnp.bfloat16), other, preferred_element_type=jnp.float32)
        if offset == 0:
            out_circ[...] = term
        else:
            out_circ[...] += term

    def circ_tile(offset):
        other = bufs[CIRC + offset]
        weights, _ = sigmoid_and_loss(score(bufs[REC], other))
        if offset == 0:
            weights = weights - diagonal()
        term = jnp.dot(weights.astype(jnp.bfloat16), other, preferred_element_type=jnp.float32)
        if offset == 0:
            out_rec[...] = term
        else:
            out_rec[...] += term

    def hard_tile(k):
        other = group[k]
        scores = score(bufs[CIRC], other)
        sigmoids, losses = sigmoid_and_loss(scores)
        first = (me * rep_count + (my_rep + k) % rep_count) * rows
        named = lax.broadcasted_iota(jnp.int32, (rows, rows), 1) + first
        times = jnp.zeros((rows, rows), jnp.float32)
        for entry in range(ids_ref.shape[1]):
            times = times + jnp.where(ids_ref[:, entry : entry + 1] == named, 1.0, 0.0)
        add_sums(times * sigmoids, scores, times * losses)
        narrow = times * sigmoids.astype(jnp.bfloat16).astype(jnp.float32)
        out_circ[...] += jnp.dot(
            narrow.astype(jnp.bfloat16), other, preferred_element_type=jnp.float32
        )

    def forward_two(c):
        arrived(REC + 2, c)
        transfer(*rec_four, c).start()
        transfer(*swap_rec, c).start()
        arrived(CIRC + 2, c)
        transfer(*circ_four, c).start()
        transfer(*swap_circ, c).start()

    def forward_four(c):
        arrived(even * (REC + 4) + odd * (CIRC + 4), c)
        transfer(*swap_last, c).start()
        arrived(odd * (REC + 4) + even * (CIRC + 4), c)

    rec_tile(0)
    forward_two(0)
    circ_tile(0)
    forward_two(1)
    hard_tile(0)
    forward_two(2)
    forward_two(3)
    rec_tile(2)
    forward_four(0)
    circ_tile(2)
    forward_four(1)

    @pl.loop(1, rep_count)
    def _(k):
        group_copy(rep_count - k).wait_recv()
        hard_tile(k)

    forward_four(2)
    forward_four(3)
    for c in range(CHUNKS):
        arrived(REC + 1, c)
        arrived(CIRC + 1, c)
    rec_tile(1)
    circ_tile(1)
    rec_tile(4)
    circ_tile(4)
    for c in range(CHUNKS):
        arrived(CIRC + 3, c)
    circ_tile(3)

    gain_part = jnp.zeros((1, rec_ref.shape[1]), jnp.float32)
    for c in range(CHUNKS):
        part = pl.ds(c * step, step)
        values = rec_ref[part].astype(jnp.float32)
        inverse = inv_rec[part]
        unit = values * gain_ref[...] * inverse
        grad = out_rec[part] * multiplier
        along = jnp.sum(unit * grad, axis=-1, keepdims=True)
        grad = (grad - unit * along) * inverse
        gain_part = gain_part + jnp.sum(values * grad, axis=0, keepdims=True)
        out_rec[part] = grad * gain_ref[...]

    for c in range(CHUNKS):
        arrived(REC + 3, c)
    rec_tile(3)

    lane = lax.broadcasted_iota(jnp.int32, (1, rec_ref.shape[1]), 1)
    totals = jnp.sum(sums[...], axis=-1, keepdims=True)
    packed = jnp.zeros((1, rec_ref.shape[1]), jnp.float32)
    for entry in range(3):
        packed = packed + jnp.where(lane == entry, totals[entry : entry + 1], 0.0)
    red_rep[my_rep, 0:1] = gain_part
    red_rep[my_rep, 1:2] = packed

    def rep_copy(k, slot):
        return pltpu.make_async_remote_copy(
            src_ref=red_rep.at[slot],
            dst_ref=red_rep.at[slot],
            send_sem=rep_send.at[k],
            recv_sem=rep_recv.at[k],
            device_id={"rep": (my_rep + k) % rep_count},
            device_id_type=MESH,
        )

    def dp_copy(k, slot):
        return pltpu.make_async_remote_copy(
            src_ref=red_dp.at[slot],
            dst_ref=red_dp.at[slot],
            send_sem=dp_send.at[k],
            recv_sem=dp_recv.at[k],
            device_id={"dp": (me + k) % loop_count},
            device_id_type=MESH,
        )

    @pl.loop(1, rep_count)
    def _(k):
        rep_copy(k, my_rep).start()

    for c in range(CHUNKS):
        part = pl.ds(c * step, step)
        inverse = inv_circ[part]
        unit = circ_ref[part].astype(jnp.float32) * inverse
        grad = out_circ[part] * multiplier
        along = jnp.sum(unit * grad, axis=-1, keepdims=True)
        out_circ[part] = (grad - unit * along) * inverse

    @pl.loop(1, rep_count)
    def _(k):
        rep_copy(k, (my_rep + rep_count - k) % rep_count).wait_recv()

    red_dp[me] = jnp.sum(red_rep[...], axis=0)

    @pl.loop(1, loop_count)
    def _(k):
        dp_copy(k, me).start()

    for message in messages:
        for c in range(CHUNKS):
            transfer(*message, c).wait_send()

    @pl.loop(1, rep_count)
    def _(k):
        group_copy(k).wait_send()
        rep_copy(k, my_rep).wait_send()

    @pl.loop(1, loop_count)
    def _(k):
        dp_copy(k, (me + loop_count - k) % loop_count).wait_recv()

    final = jnp.sum(red_dp[...], axis=0)
    out_gain[...] = final[0:1]
    out_stat[...] = final[1:2, 0:2]
    out_loss[...] = final[1:2, 2:3] * (1.0 / (rows * loop_count * rep_count))

    @pl.loop(1, loop_count)
    def _(k):
        dp_copy(k, me).wait_send()


def per_device(loop_count, rep_count, circuits, records, record_gain, log_scale, logit_bias, ids):
    rows, width = circuits.shape
    vmem = pl.BlockSpec(memory_space=pltpu.VMEM)
    smem = pl.BlockSpec(memory_space=pltpu.SMEM)
    dma = pltpu.SemaphoreType.DMA
    grad_circuits, grad_records, gain, stat, loss = pl.pallas_call(
        functools.partial(kernel, loop_count, rep_count),
        out_shape=(
            jax.ShapeDtypeStruct((rows, width), jnp.float32),
            jax.ShapeDtypeStruct((rows, width), jnp.float32),
            jax.ShapeDtypeStruct((1, width), jnp.float32),
            jax.ShapeDtypeStruct((1, 2), jnp.float32),
            jax.ShapeDtypeStruct((1, 1), jnp.float32),
        ),
        in_specs=[vmem, vmem, vmem, smem, smem, vmem],
        out_specs=(vmem,) * 5,
        scratch_shapes=[
            pltpu.VMEM((10, rows, width), jnp.bfloat16),
            pltpu.VMEM((rep_count, rows, width), jnp.bfloat16),
            pltpu.VMEM((rows, 1), jnp.float32),
            pltpu.VMEM((rows, 1), jnp.float32),
            pltpu.VMEM((3, rows), jnp.float32),
            pltpu.VMEM((rep_count, 2, width), jnp.float32),
            pltpu.VMEM((loop_count, 2, width), jnp.float32),
            dma((8, CHUNKS)),
            dma((10, CHUNKS)),
            dma((rep_count,)),
            dma((rep_count,)),
            dma((rep_count,)),
            dma((rep_count,)),
            dma((loop_count,)),
            dma((loop_count,)),
        ],
        compiler_params=pltpu.CompilerParams(
            collective_id=0, has_side_effects=True, vmem_limit_bytes=48 * 1024 * 1024
        ),
    )(circuits, records, record_gain.reshape(1, width), log_scale, logit_bias, ids)
    return (grad_circuits, grad_records, gain.reshape(width), stat.reshape(2), loss.reshape(1))


def solution(mesh):
    split = P(("dp", "rep"), None)
    return jax.shard_map(
        functools.partial(per_device, mesh.shape["dp"], mesh.shape["rep"]),
        mesh=mesh,
        in_specs=(split, split, P(), P(), P(), split),
        out_specs=(split, split, P(), P(), P()),
        check_vma=False,
    )
```
